32 devices in a mesh: sub: 4 (over y, x), clu: 8 (over z, core).
Axes of the slice: x: 2, y: 2, z: 4, core: 2. Of those that a mesh axis runs over, the one named last changes fastest.
Arguments:
- right_side: float32 [65536, 256], P(('sub', 'clu')), may hold values from -6 to 6
- near_blocks: float32 [128, 3, 512, 512], P(('sub', 'clu')), may hold values from -0.15625 to 0.15625
- near_index: int32 [128, 3], P(('sub', 'clu')), may hold values from 0 to 127, as said below
- bases: float32 [128, 512, 128], P(('sub', 'clu')), may hold values from -0.25 to 0.25
- leaf_transfer: float32 [128, 128, 128], P(('sub', 'clu')), may hold values from -0.25 to 0.25
- cluster_transfer: float32 [32, 128, 128], P(('sub', 'clu')), may hold values from -0.1875 to 0.1875
- cluster_coupling: float32 [32, 4, 128, 128], P(('sub', 'clu')), may hold values from -0.25 to 0.25
- cluster_list: int32 [32, 4], P(('sub', 'clu')), may hold values from 0 to 31, as said below
- subtree_coupling: float32 [4, 3, 128, 128], P('sub'), may hold values from -0.3125 to 0.3125
- subtree_list: int32 [4, 3], P('sub'), may hold values from 0 to 3, as said below
Outputs:
- solution: float32 [65536, 256], P(('sub', 'clu'))
- residual: float32 [65536, 256], P(('sub', 'clu'))
The draws below stay inside these ranges and needn't reach their ends.
Inputs may be any that keep to these rules, and one draw needn't show every extreme that they name: `near_index`: row g begins with g itself; its other entries are two different leaves within 2 leaves of g held by the same subtree; the first leaf of a cluster names the leaf before it, and the last the leaf after it, where those lie in the same subtree. `cluster_list`: the entries of a row are different clusters of the same subtree as the row's cluster, never that cluster itself. `subtree_list`: the entries of a row are different subtrees, never the row's own.
All inputs are finite; a program needn't handle non-finite values.
Results may differ from the reference program's by a relative error of at most 0.0001.
Values sent between devices are 32-bit elements; how exact they have to be, the bound alone decides.
A program may use at most 128 MiB of HBM per device.

```python
import jax
import jax.numpy as jnp
from jax import lax

LEAF = 512
RANK = 128
RHS = 256
NEAR = 3
NCC = 4
NSC = 3
ITERS = 3
LEAF_DEV = 4
CLUSTERS = 32
SUBTREES = 4
LEAVES = 128
ROWS = 65536


def draw_near_index(key, part):
    leaf_ids = jnp.arange(LEAVES, dtype=jnp.int32)
    offsets = jnp.array([-2, -1, 1, 2], dtype=jnp.int32)
    targets = leaf_ids[:, None] + offsets[None, :]
    span = LEAF_DEV * (CLUSTERS // SUBTREES)
    valid = (targets >= 0) & (targets < LEAVES) & (targets // span == leaf_ids[:, None] // span)
    scores = jax.random.randint(key, (LEAVES, 4), 0, 1000, dtype=jnp.int32) * 8 + jnp.arange(4, dtype=jnp.int32)[None, :]
    position = leaf_ids % LEAF_DEV
    forced = (position[:, None] == 0) & (offsets[None, :] == -1) | (position[:, None] == LEAF_DEV - 1) & (offsets[None, :] == 1)
    scores = scores + jnp.where(forced, 100000, 0)
    scores = jnp.where(valid, scores, -10000000)
    order = jnp.argsort(-scores, axis=1, stable=True)[:, :2]
    chosen = jnp.take_along_axis(targets, order, axis=1)
    return jnp.concatenate([leaf_ids[:, None], chosen], axis=1).astype(jnp.int32)


def draw_cluster_list(key, part):
    per_subtree = CLUSTERS // SUBTREES
    cluster_ids = jnp.arange(CLUSTERS, dtype=jnp.int32)
    local_ids = jnp.arange(per_subtree, dtype=jnp.int32)
    scores = jax.random.randint(jax.random.fold_in(key, 7), (CLUSTERS, per_subtree), 0, 1000, dtype=jnp.int32) * per_subtree + local_ids[None, :]
    scores = jnp.where(local_ids[None, :] == (cluster_ids % per_subtree)[:, None], -1000000, scores)
    order = jnp.argsort(-scores, axis=1, stable=True)[:, :NCC].astype(jnp.int32)
    return ((cluster_ids // per_subtree)[:, None] * per_subtree + order).astype(jnp.int32)


def draw_subtree_list(key, part):
    subtree_ids = jnp.arange(SUBTREES, dtype=jnp.int32)
    scores = jax.random.randint(jax.random.fold_in(key, 11), (SUBTREES, SUBTREES), 0, 1000, dtype=jnp.int32) * SUBTREES + subtree_ids[None, :]
    scores = jnp.where(subtree_ids[None, :] == subtree_ids[:, None], -1000000, scores)
    return jnp.argsort(-scores, axis=1, stable=True)[:, :NSC].astype(jnp.int32)


def levels(key, extent, cuts, smallest, high):
    loudness = 1.0
    for axis_at, shards_of in cuts:
        steps = jax.random.uniform(jax.random.fold_in(jax.random.fold_in(key, 6), axis_at), (shards_of,), jnp.float32, smallest / len(cuts), high / len(cuts))
        loudness = loudness * jnp.repeat(jnp.exp(steps), extent[axis_at] // shards_of).reshape((-1,) + (1,) * (len(extent) - 1 - axis_at))
    return loudness


def bell_draw(stream_key, extent, scale, most, shards=(), held_as=jnp.bfloat16):
    factor_of = levels(stream_key, extent, shards, -0.22, 0.18) if shards else 1.0
    values = jax.random.normal(stream_key, extent, jnp.float32) * scale * factor_of
    return jnp.minimum(jnp.maximum(values, -most), most).astype(held_as)


def setup_inputs(seed: int = 0) -> dict:
    splits = jax.random.split(jax.random.key(seed), 11)
    return {
        "right_side": bell_draw(splits[0], (ROWS, RHS), 1.0, 6.0, ((0, 32),), jnp.float32),
        "near_blocks": bell_draw(splits[1], (LEAVES, NEAR, LEAF, LEAF), (LEAF * NEAR) ** -0.5, 0.15625, ((0, 32),), jnp.float32),
        "near_index": draw_near_index(jax.random.fold_in(splits[10], 71), 0),
        "bases": bell_draw(splits[3], (LEAVES, LEAF, RANK), LEAF ** -0.5, 0.25, ((0, 32),), jnp.float32),
        "leaf_transfer": bell_draw(splits[4], (LEAVES, RANK, RANK), (RANK * LEAF_DEV) ** -0.5, 0.25, ((0, 32),), jnp.float32),
        "cluster_transfer": bell_draw(splits[5], (CLUSTERS, RANK, RANK), (RANK * CLUSTERS // SUBTREES) ** -0.5, 0.1875, ((0, 32),), jnp.float32),
        "cluster_coupling": bell_draw(splits[6], (CLUSTERS, NCC, RANK, RANK), (RANK * NCC) ** -0.5, 0.25, ((0, 32),), jnp.float32),
        "cluster_list": draw_cluster_list(jax.random.fold_in(splits[10], 71), 0),
        "subtree_coupling": bell_draw(splits[8], (SUBTREES, NSC, RANK, RANK), (RANK * NSC) ** -0.5, 0.3125, ((0, 4),), jnp.float32),
        "subtree_list": draw_subtree_list(jax.random.fold_in(splits[10], 71), 0),
    }


highest = lax.Precision.HIGHEST
spectrum_center = 3.0
spectrum_radius = 2.0
ridge_shift = 3.0


def near_field(vector_in, near_blocks, near_index):
    leaves = vector_in.reshape(LEAVES, LEAF, RHS)

    def one_leaf(pair):
        blocks, picks = pair
        return jnp.einsum('jab,jbr->ar', blocks, leaves[picks], precision=highest)

    return lax.map(one_leaf, (near_blocks, near_index)).reshape(ROWS, RHS)


def far_field(vector_in, bases, leaf_transfer, cluster_transfer, cluster_coupling, cluster_list, subtree_coupling, subtree_list):
    per_subtree = CLUSTERS // SUBTREES
    leaves = vector_in.reshape(LEAVES, LEAF, RHS)
    leaf_coeffs = jnp.einsum('lak,lar->lkr', bases, leaves, precision=highest)
    grouped = leaf_coeffs.reshape(CLUSTERS, LEAF_DEV, RANK, RHS)
    transfers = leaf_transfer.reshape(CLUSTERS, LEAF_DEV, RANK, RANK)
    cluster_coeffs = jnp.einsum('dlkm,dlkr->dmr', transfers, grouped, precision=highest)
    upper = cluster_transfer.reshape(SUBTREES, per_subtree, RANK, RANK)
    subtree_coeffs = jnp.einsum('scka,sckr->sar', upper, cluster_coeffs.reshape(SUBTREES, per_subtree, RANK, RHS), precision=highest)
    cluster_far = jnp.einsum('djab,djbr->dar', cluster_coupling, cluster_coeffs[cluster_list], precision=highest)
    subtree_far = jnp.einsum('sjab,sjbr->sar', subtree_coupling, subtree_coeffs[subtree_list], precision=highest)
    spread = jnp.einsum('scka,sar->sckr', upper, subtree_far, precision=highest).reshape(CLUSTERS, RANK, RHS)
    combined = cluster_far + spread
    lowered = jnp.einsum('dlkm,dmr->dlkr', transfers, combined, precision=highest).reshape(LEAVES, RANK, RHS)
    return jnp.einsum('lak,lkr->lar', bases, lowered, precision=highest).reshape(ROWS, RHS)


def reference(right_side, near_blocks, near_index, bases, leaf_transfer, cluster_transfer, cluster_coupling, cluster_list, subtree_coupling, subtree_list):
    def operator(vector_in):
        near = near_field(vector_in, near_blocks, near_index)
        far = far_field(vector_in, bases, leaf_transfer, cluster_transfer, cluster_coupling, cluster_list, subtree_coupling, subtree_list)
        return ridge_shift * vector_in + near + far

    solution = jnp.zeros_like(right_side)
    residual = right_side
    update = right_side / spectrum_center
    weight_old = spectrum_radius / spectrum_center
    for turn_index in range(ITERS):
        solution = solution + update
        residual = residual - operator(update)
        if turn_index + 1 < ITERS:
            weight_new = 1.0 / (2.0 * spectrum_center / spectrum_radius - weight_old)
            update = (weight_new * weight_old) * update + (2.0 * weight_new / spectrum_radius) * residual
            weight_old = weight_new
    return solution, residual
```

```python
import jax
import jax.numpy as jnp
from jax import lax
from jax.experimental import pallas as pl
from jax.experimental.pallas import tpu as pltpu
from jax.sharding import PartitionSpec as P

REACH = 2
ITERS = 3

spectrum_center = 3.0
spectrum_radius = 2.0
ridge_shift = 3.0

MESH = pl.DeviceIdType.MESH


def step_weights():
    weights = []
    old = spectrum_radius / spectrum_center
    for _ in range(ITERS - 1):
        new = 1.0 / (2.0 * spectrum_center / spectrum_radius - old)
        weights.append((new * old, 2.0 * new / spectrum_radius))
        old = new
    return weights


def split(x):
    high = x.astype(jnp.bfloat16)
    return high, (x - high.astype(jnp.float32)).astype(jnp.bfloat16)


def dot3(ah, al, bh, bl):
    def dot(a, b):
        return jnp.dot(a, b, preferred_element_type=jnp.float32)

    return dot(ah, bh) + (dot(ah, bl) + dot(al, bh))


def kernel(
    n_clu,
    n_sub,
    near_index,
    cluster_list,
    subtree_list,
    right_side,
    near_blocks,
    bases,
    leaf_transfer,
    cluster_transfer,
    cluster_coupling,
    subtree_coupling,
    solution,
    residual,
    update,
    halo,
    win_h,
    win_l,
    stage,
    near_h,
    near_l,
    w_h,
    w_l,
    wt_h,
    wt_l,
    t_all,
    tt_h,
    tt_l,
    coeffs,
    g_h,
    g_l,
    sub_all,
    s_h,
    s_l,
    c_far,
    stage_sem,
    halo_send,
    halo_recv,
    t_send,
    t_recv,
    c_send,
    c_recv,
    sub_send,
    sub_recv,
):
    leaf_count, leaf_rows, rank = bases.shape
    near_count = near_index.shape[1]
    ncc = cluster_list.shape[1]
    nsc = subtree_list.shape[1]
    sub = lax.axis_index("sub")
    clu = lax.axis_index("clu")
    lane = lax.rem(clu, 2)
    partner = clu + 1 - 2 * lane
    places = n_clu // 2
    has_low, has_high = clu >= 1, clu + 1 < n_clu
    has_down, has_up = clu >= 2, clu + 2 < n_clu
    first_leaf = (sub * n_clu + clu) * leaf_count

    barrier = pltpu.get_barrier_semaphore()

    def greet(device):
        pl.semaphore_signal(barrier, inc=1, device_id=device, device_id_type=MESH)

    for ok, where in ((has_low, clu - 1), (has_high, clu + 1), (has_down, clu - 2), (has_up, clu + 2)):

        @pl.when(ok)
        def _():
            greet({"clu": where})

    for k in range(1, n_sub):
        greet({"sub": lax.rem(sub + k, n_sub)})
    count = n_sub - 1
    for ok in (has_low, has_high, has_down, has_up):
        count = count + jnp.where(ok, 1, 0)
    pl.semaphore_wait(barrier, count)

    def stage_copy(i):
        slot = lax.rem(i, 2)
        return pltpu.make_async_copy(
            near_blocks.at[i // near_count, lax.rem(i, near_count)], stage.at[slot], stage_sem.at[slot]
        )

    stage_copy(0).start()
    stage_copy(1).start()

    class Chain:
        def __init__(self, view, send, recv):
            self.view, self.send, self.recv = view, send, recv

        def copy(self, block, way, target):
            return pltpu.make_async_remote_copy(
                src_ref=self.view(block),
                dst_ref=self.view(block),
                send_sem=self.send.at[way, block],
                recv_sem=self.recv(block),
                device_id={"clu": target},
                device_id_type=MESH,
            )

        def begin(self):
            @pl.when(has_up)
            def _():
                self.copy(clu, 0, clu + 2).start()

            @pl.when(has_down)
            def _():
                self.copy(clu, 1, clu - 2).start()

            self.copy(clu, 2, partner).start()

        def relay(self, t):
            @pl.when(clu - 2 * t >= 0)
            def _():
                block = clu - 2 * t
                self.copy(block, 2, partner).wait_recv()

                @pl.when(has_up)
                def _():
                    self.copy(block, 0, clu + 2).start()

                self.copy(block, 2, partner).start()

            @pl.when(clu + 2 * t < n_clu)
            def _():
                block = clu + 2 * t
                self.copy(block, 2, partner).wait_recv()

                @pl.when(has_down)
                def _():
                    self.copy(block, 1, clu - 2).start()

                self.copy(block, 2, partner).start()

        def finish(self):
            for q in range(places):
                self.copy(2 * q + 1 - lane, 2, partner).wait_recv()

        def drain(self):
            for q in range(places):
                block = 2 * q + lane

                @pl.when((block <= clu) & has_up)
                def _():
                    self.copy(block, 0, clu + 2).wait_send()

                @pl.when((block >= clu) & has_down)
                def _():
                    self.copy(block, 1, clu - 2).wait_send()

                self.copy(block, 2, partner).wait_send()

    t_chain = Chain(lambda b: t_all.at[b], t_send, lambda b: t_recv.at[b])

    def c_chain(it):
        return Chain(lambda b: coeffs.at[it, b], c_send, lambda b: c_recv.at[it, b])

    def halo_copy(it, side):
        return pltpu.make_async_remote_copy(
            src_ref=update.at[pl.ds(leaf_count - REACH if side == 0 else 0, REACH)],
            dst_ref=halo.at[it, side],
            send_sem=halo_send.at[side],
            recv_sem=halo_recv.at[it, side],
            device_id={"clu": clu + 1 if side == 0 else clu - 1},
            device_id_type=MESH,
        )

    def halo_start(it):
        @pl.when(has_high)
        def _():
            halo_copy(it, 0).start()

        @pl.when(has_low)
        def _():
            halo_copy(it, 1).start()

    def send_coeffs(it):
        total = None
        for leaf in range(leaf_count):
            term = dot3(wt_h[leaf], wt_l[leaf], win_h[REACH + leaf], win_l[REACH + leaf])
            total = term if total is None else total + term
        coeffs[it, clu] = total
        c_chain(it).begin()

    def first(leaf, carry):
        rows = pl.ds(leaf * leaf_rows, leaf_rows)
        r = right_side[rows, :]
        u = r / spectrum_center
        residual[rows, :] = r
        solution[rows, :] = u
        update[leaf] = u
        win_h[REACH + leaf], win_l[REACH + leaf] = split(u)
        return carry

    lax.fori_loop(0, leaf_count, first, 0)
    halo_start(0)
    t_all[clu] = cluster_transfer[0]
    t_chain.begin()

    def fold(leaf, carry):
        bh, bl = split(bases[leaf])
        lh, ll = split(leaf_transfer[leaf])
        w = dot3(bh, bl, lh, ll)
        w_h[leaf], w_l[leaf] = split(w)
        wt_h[leaf], wt_l[leaf] = split(w.T)
        return carry

    lax.fori_loop(0, leaf_count, fold, 0)
    send_coeffs(0)

    def unpack(i, carry):
        stage_copy(i).wait()
        near_h[i], near_l[i] = split(stage[lax.rem(i, 2)])

        @pl.when(i + 2 < leaf_count * near_count)
        def _():
            stage_copy(i + 2).start()

        return carry

    lax.fori_loop(0, leaf_count * near_count, unpack, 0)
    for t in range(1, places):
        t_chain.relay(t)
    t_chain.finish()
    for b in range(n_clu):
        tt_h[:, b * rank : (b + 1) * rank], tt_l[:, b * rank : (b + 1) * rank] = split(t_all[b].T)
    t_chain.drain()

    weights = step_weights()

    def near_product(leaf, j, where):
        i = leaf * near_count + j
        return dot3(near_h[i], near_l[i], win_h[where], win_l[where])

    def sub_copy(it, k, owner, target):
        return pltpu.make_async_remote_copy(
            src_ref=sub_all.at[it, owner],
            dst_ref=sub_all.at[it, owner],
            send_sem=sub_send.at[k],
            recv_sem=sub_recv.at[it, owner],
            device_id={"sub": target},
            device_id_type=MESH,
        )

    def iteration(it, carry):
        chain = c_chain(it)

        def own(leaf, carry):
            rows = pl.ds(leaf * leaf_rows, leaf_rows)
            residual[rows, :] = residual[rows, :] - (
                ridge_shift * update[leaf] + near_product(leaf, 0, REACH + leaf)
            )
            return carry

        chain.relay(1)
        lax.fori_loop(0, leaf_count, own, 0)
        for t in range(2, places):
            chain.relay(t)
        chain.finish()
        for b in range(n_clu):
            g_h[b], g_l[b] = split(coeffs[it, b])
        flat = (n_clu * rank, g_h.shape[2])
        sub_all[it, sub] = dot3(
            tt_h[...], tt_l[...], g_h[...].reshape(flat), g_l[...].reshape(flat)
        )
        for k in range(1, n_sub):
            sub_copy(it, k, sub, lax.rem(sub + k, n_sub)).start()
        far = None
        for j in range(ncc):
            at = jnp.clip(cluster_list[0, j] - sub * n_clu, 0, n_clu - 1)
            ah, al = split(cluster_coupling[0, j])
            term = dot3(ah, al, g_h[at], g_l[at])
            far = term if far is None else far + term
        c_far[...] = far

        @pl.when(has_low)
        def _():
            halo_copy(it, 0).wait_recv()
            for k in range(REACH):
                win_h[k], win_l[k] = split(halo[it, 0, k])

        @pl.when(has_high)
        def _():
            halo_copy(it, 1).wait_recv()
            for k in range(REACH):
                at = REACH + leaf_count + k
                win_h[at], win_l[at] = split(halo[it, 1, k])

        def others(leaf, carry):
            rows = pl.ds(leaf * leaf_rows, leaf_rows)
            total = None
            for j in range(1, near_count):
                where = jnp.clip(near_index[leaf, j] - first_leaf + REACH, 0, win_h.shape[0] - 1)
                term = near_product(leaf, j, where)
                total = term if total is None else total + term
            residual[rows, :] = residual[rows, :] - total
            return carry

        lax.fori_loop(0, leaf_count, others, 0)

        for k in range(1, n_sub):
            owner = lax.rem(sub + k, n_sub)
            sub_copy(it, k, owner, owner).wait_recv()
        for s in range(n_sub):
            s_h[s], s_l[s] = split(sub_all[it, s])
        top = None
        for j in range(nsc):
            at = subtree_list[0, j]
            ah, al = split(subtree_coupling[0, j])
            term = dot3(ah, al, s_h[at], s_l[at])
            top = term if top is None else top + term
        th, tl = split(top)
        ch, cl = split(cluster_transfer[0])
        down_h, down_l = split(c_far[...] + dot3(ch, cl, th, tl))
        for leaf in range(leaf_count):
            rows = pl.ds(leaf * leaf_rows, leaf_rows)
            residual[rows, :] = residual[rows, :] - dot3(w_h[leaf], w_l[leaf], down_h, down_l)

        chain.drain()
        for k in range(1, n_sub):
            sub_copy(it, k, sub, lax.rem(sub + k, n_sub)).wait_send()

        @pl.when(has_high)
        def _():
            halo_copy(it, 0).wait_send()

        @pl.when(has_low)
        def _():
            halo_copy(it, 1).wait_send()

        @pl.when(it + 1 < ITERS)
        def _():
            keep, gain = weights[-1]
            for k in range(len(weights) - 1):
                keep = jnp.where(it == k, weights[k][0], keep)
                gain = jnp.where(it == k, weights[k][1], gain)

            def advance(leaf, carry):
                rows = pl.ds(leaf * leaf_rows, leaf_rows)
                u = keep * update[leaf] + gain * residual[rows, :]
                update[leaf] = u
                solution[rows, :] = solution[rows, :] + u
                win_h[REACH + leaf], win_l[REACH + leaf] = split(u)
                return carry

            lax.fori_loop(0, leaf_count, advance, 0)
            send_coeffs(it + 1)
            halo_start(it + 1)

        return carry

    lax.fori_loop(0, ITERS, iteration, 0)


def body(
    right_side,
    near_blocks,
    near_index,
    bases,
    leaf_transfer,
    cluster_transfer,
    cluster_coupling,
    cluster_list,
    subtree_coupling,
    subtree_list,
):
    n_clu, n_sub = lax.axis_size("clu"), lax.axis_size("sub")
    leaf_count, leaf_rows, rank = bases.shape
    columns = right_side.shape[1]
    near_count = near_index.shape[1]
    blocks = leaf_count * near_count
    wide = leaf_count + 2 * REACH
    f32, bf16 = jnp.float32, jnp.bfloat16
    vmem = pl.BlockSpec(memory_space=pltpu.VMEM)
    smem = pl.BlockSpec(memory_space=pltpu.SMEM)
    hbm = pl.BlockSpec(memory_space=pl.ANY)
    dma = pltpu.SemaphoreType.DMA

    def run(*args):
        return kernel(n_clu, n_sub, *args)

    return pl.pallas_call(
        run,
        out_shape=(
            jax.ShapeDtypeStruct(right_side.shape, f32),
            jax.ShapeDtypeStruct(right_side.shape, f32),
        ),
        in_specs=[smem] * 3 + [vmem, hbm] + [vmem] * 5,
        out_specs=(vmem, vmem),
        scratch_shapes=[
            pltpu.VMEM((leaf_count, leaf_rows, columns), f32),
            pltpu.VMEM((ITERS, 2, REACH, leaf_rows, columns), f32),
            pltpu.VMEM((wide, leaf_rows, columns), bf16),
            pltpu.VMEM((wide, leaf_rows, columns), bf16),
            pltpu.VMEM((2, leaf_rows, leaf_rows), f32),
            pltpu.VMEM((blocks, leaf_rows, leaf_rows), bf16),
            pltpu.VMEM((blocks, leaf_rows, leaf_rows), bf16),
            pltpu.VMEM((leaf_count, leaf_rows, rank), bf16),
            pltpu.VMEM((leaf_count, leaf_rows, rank), bf16),
            pltpu.VMEM((leaf_count, rank, leaf_rows), bf16),
            pltpu.VMEM((leaf_count, rank, leaf_rows), bf16),
            pltpu.VMEM((n_clu, rank, rank), f32),
            pltpu.VMEM((rank, n_clu * rank), bf16),
            pltpu.VMEM((rank, n_clu * rank), bf16),
            pltpu.VMEM((ITERS, n_clu, rank, columns), f32),
            pltpu.VMEM((n_clu, rank, columns), bf16),
            pltpu.VMEM((n_clu, rank, columns), bf16),
            pltpu.VMEM((ITERS, n_sub, rank, columns), f32),
            pltpu.VMEM((n_sub, rank, columns), bf16),
            pltpu.VMEM((n_sub, rank, columns), bf16),
            pltpu.VMEM((rank, columns), f32),
            dma((2,)),
            dma((2,)),
            dma((ITERS, 2)),
            dma((3, n_clu)),
            dma((n_clu,)),
            dma((3, n_clu)),
            dma((ITERS, n_clu)),
            dma((n_sub,)),
            dma((ITERS, n_sub)),
        ],
        compiler_params=pltpu.CompilerParams(
            collective_id=0, has_side_effects=True, vmem_limit_bytes=63_000_000
        ),
    )(
        near_index,
        cluster_list,
        subtree_list,
        right_side,
        near_blocks,
        bases,
        leaf_transfer,
        cluster_transfer,
        cluster_coupling,
        subtree_coupling,
    )


def solution(mesh):
    placed = (
        P(("sub", "clu"), None),
        P(("sub", "clu"), None, None, None),
        P(("sub", "clu"), None),
        P(("sub", "clu"), None, None),
        P(("sub", "clu"), None, None),
        P(("sub", "clu"), None, None),
        P(("sub", "clu"), None, None, None),
        P(("sub", "clu"), None),
        P("sub", None, None, None),
        P("sub", None),
    )
    return jax.shard_map(
        body,
        mesh=mesh,
        in_specs=placed,
        out_specs=(P(("sub", "clu"), None), P(("sub", "clu"), None)),
        check_vma=False,
    )
```

```python
import jax
import jax.numpy as jnp
from jax import lax
from jax.experimental import pallas as pl
from jax.experimental.pallas import tpu as pltpu
from jax.sharding import PartitionSpec as P

REACH = 2
ITERS = 3
PIECES = 1
HALO_PIECES = 8

spectrum_center = 3.0
spectrum_radius = 2.0
ridge_shift = 3.0

MESH = pl.DeviceIdType.MESH


def step_weights():
    weights = []
    old = spectrum_radius / spectrum_center
    for _ in range(ITERS - 1):
        new = 1.0 / (2.0 * spectrum_center / spectrum_radius - old)
        weights.append((new * old, 2.0 * new / spectrum_radius))
        old = new
    return weights


def split(x):
    high = x.astype(jnp.bfloat16)
    return high, (x - high.astype(jnp.float32)).astype(jnp.bfloat16)


def dot3(ah, al, bh, bl):
    def dot(a, b):
        return jnp.dot(a, b, preferred_element_type=jnp.float32)

    return dot(ah, bh) + (dot(ah, bl) + dot(al, bh))


def kernel(
    n_clu,
    n_sub,
    near_index,
    cluster_list,
    subtree_list,
    right_side,
    near_blocks,
    bases,
    leaf_transfer,
    cluster_transfer,
    cluster_coupling,
    subtree_coupling,
    solution,
    residual,
    update,
    halo,
    win_h,
    win_l,
    stage,
    near_h,
    near_l,
    w_h,
    w_l,
    wt_h,
    wt_l,
    t_all,
    tt_h,
    tt_l,
    coeffs,
    g_h,
    g_l,
    sub_all,
    s_h,
    s_l,
    c_far,
    c_near,
    gram,
    down_h,
    down_l,
    pending,
    w_own,
    w_beside,
    wb_h,
    wb_l,
    down_own,
    down_beside,
    stage_sem,
    halo_send,
    halo_recv,
    t_send,
    t_recv,
    c_send,
    c_recv,
    sub_send,
    sub_recv,
    w_send,
    w_recv,
    down_send,
    down_recv,
):
    leaf_count, leaf_rows, rank = bases.shape
    near_count = near_index.shape[1]
    ncc = cluster_list.shape[1]
    nsc = subtree_list.shape[1]
    sub = lax.axis_index("sub")
    clu = lax.axis_index("clu")
    lane = lax.rem(clu, 2)
    partner = clu + 1 - 2 * lane
    places = n_clu // 2
    has_low, has_high = clu >= 1, clu + 1 < n_clu
    has_down, has_up = clu >= 2, clu + 2 < n_clu
    first_leaf = (sub * n_clu + clu) * leaf_count

    barrier = pltpu.get_barrier_semaphore()

    def greet(device):
        pl.semaphore_signal(barrier, inc=1, device_id=device, device_id_type=MESH)

    for ok, where in ((has_low, clu - 1), (has_high, clu + 1), (has_down, clu - 2), (has_up, clu + 2)):

        @pl.when(ok)
        def _():
            greet({"clu": where})

    for k in range(1, n_sub):
        greet({"sub": lax.rem(sub + k, n_sub)})
    count = n_sub - 1
    for ok in (has_low, has_high, has_down, has_up):
        count = count + jnp.where(ok, 1, 0)
    pl.semaphore_wait(barrier, count)

    def stage_copy(i):
        slot = lax.rem(i, 2)
        return pltpu.make_async_copy(
            near_blocks.at[i // near_count, lax.rem(i, near_count)], stage.at[slot], stage_sem.at[slot]
        )

    stage_copy(0).start()
    stage_copy(1).start()

    class Chain:
        def __init__(self, view, send, recv):
            self.view, self.send, self.recv = view, send, recv

        def copy(self, block, piece, way, target):
            return pltpu.make_async_remote_copy(
                src_ref=self.view(block, piece),
                dst_ref=self.view(block, piece),
                send_sem=self.send.at[way, block, piece],
                recv_sem=self.recv(block, piece),
                device_id={"clu": target},
                device_id_type=MESH,
            )

        def begin(self):
            for piece in range(PIECES):

                @pl.when(has_up)
                def _():
                    self.copy(clu, piece, 0, clu + 2).start()

                @pl.when(has_down)
                def _():
                    self.copy(clu, piece, 1, clu - 2).start()

            for piece in range(PIECES):
                self.copy(clu, piece, 2, partner).start()

        def relay(self, t):
            for piece in range(PIECES):

                @pl.when(clu - 2 * t >= 0)
                def _():
                    block = clu - 2 * t
                    self.copy(block, piece, 2, partner).wait_recv()

                    @pl.when(has_up)
                    def _():
                        self.copy(block, piece, 0, clu + 2).start()

                    self.copy(block, piece, 2, partner).start()

                @pl.when(clu + 2 * t < n_clu)
                def _():
                    block = clu + 2 * t
                    self.copy(block, piece, 2, partner).wait_recv()

                    @pl.when(has_down)
                    def _():
                        self.copy(block, piece, 1, clu - 2).start()

                    self.copy(block, piece, 2, partner).start()

        def finish(self):
            for q in range(places):
                for piece in range(PIECES):
                    self.copy(2 * q + 1 - lane, piece, 2, partner).wait_recv()

        def drain(self):
            for q in range(places):
                block = 2 * q + lane
                for piece in range(PIECES):

                    @pl.when((block <= clu) & has_up)
                    def _():
                        self.copy(block, piece, 0, clu + 2).wait_send()

                    @pl.when((block >= clu) & has_down)
                    def _():
                        self.copy(block, piece, 1, clu - 2).wait_send()

                    self.copy(block, piece, 2, partner).wait_send()

    part = rank // PIECES
    t_chain = Chain(
        lambda b, p: t_all.at[b, pl.ds(p * part, part)], t_send, lambda b, p: t_recv.at[b, p]
    )

    def c_chain(it):
        return Chain(
            lambda b, p: coeffs.at[it, b, pl.ds(p * part, part)],
            c_send,
            lambda b, p: c_recv.at[it, b, p],
        )

    def edge(side):
        return pl.ds(leaf_count - REACH if side == 0 else 0, REACH)

    def beside(src, dst, send, recv, side):
        return pltpu.make_async_remote_copy(
            src_ref=src,
            dst_ref=dst,
            send_sem=send,
            recv_sem=recv,
            device_id={"clu": clu + 1 if side == 0 else clu - 1},
            device_id_type=MESH,
        )

    def w_copy(side):
        return beside(w_own.at[edge(side)], w_beside.at[side], w_send.at[side], w_recv.at[side], side)

    def down_copy(it, side):
        return beside(
            down_own.at[it],
            down_beside.at[it, side],
            down_send.at[side],
            down_recv.at[it, side],
            side,
        )

    def both_sides(act):
        @pl.when(has_high)
        def _():
            act(0)

        @pl.when(has_low)
        def _():
            act(1)

    per_leaf = HALO_PIECES // REACH
    chunk = leaf_rows // per_leaf

    def halo_copy(it, side, piece):
        k, rows = piece // per_leaf, pl.ds(piece % per_leaf * chunk, chunk)
        leaf = (leaf_count - REACH if side == 0 else 0) + k
        return beside(
            pending.at[leaf, rows],
            halo.at[it, side, k, rows],
            halo_send.at[side, piece],
            halo_recv.at[it, side, piece],
            side,
        )

    def halo_start(it, group):
        begin, end = HALO_PIECES * group // places, HALO_PIECES * (group + 1) // places

        def start(side):
            for piece in range(begin, end):
                halo_copy(it, side, piece).start()

        both_sides(start)

    def own_coeffs():
        total = None
        for leaf in range(leaf_count):
            term = dot3(wt_h[leaf], wt_l[leaf], win_h[REACH + leaf], win_l[REACH + leaf])
            total = term if total is None else total + term
        return total

    def first(leaf, carry):
        rows = pl.ds(leaf * leaf_rows, leaf_rows)
        r = right_side[rows, :]
        u = r / spectrum_center
        residual[rows, :] = r
        solution[rows, :] = u
        update[leaf] = u
        pending[leaf] = u
        win_h[REACH + leaf], win_l[REACH + leaf] = split(u)
        return carry

    lax.fori_loop(0, leaf_count, first, 0)
    t_all[clu] = cluster_transfer[0]
    t_chain.begin()
    halo_start(0, 0)

    def fold(leaf, carry):
        bh, bl = split(bases[leaf])
        lh, ll = split(leaf_transfer[leaf])
        w = dot3(bh, bl, lh, ll)
        w_own[leaf] = w
        w_h[leaf], w_l[leaf] = split(w)
        wt_h[leaf], wt_l[leaf] = split(w.T)
        gram[...] += dot3(wt_h[leaf], wt_l[leaf], w_h[leaf], w_l[leaf])
        return carry

    gram[...] = jnp.zeros_like(gram)
    lax.fori_loop(0, leaf_count, fold, 0)
    coeffs[0, clu] = own_coeffs()
    c_chain(0).begin()

    def unpack(i, carry):
        stage_copy(i).wait()
        near_h[i], near_l[i] = split(stage[lax.rem(i, 2)])

        @pl.when(i + 2 < leaf_count * near_count)
        def _():
            stage_copy(i + 2).start()

        return carry

    blocks = leaf_count * near_count
    for t in range(1, places):
        halo_start(0, t)
        lax.fori_loop(blocks * (t - 1) // (places - 1), blocks * t // (places - 1), unpack, 0)
        t_chain.relay(t)
        c_chain(0).relay(t)
    t_chain.finish()
    for b in range(n_clu):
        tt_h[:, b * rank : (b + 1) * rank], tt_l[:, b * rank : (b + 1) * rank] = split(t_all[b].T)
    t_chain.drain()

    weights = step_weights()

    def pick_weight(it, which):
        value = weights[-1][which]
        for k in range(len(weights) - 1):
            value = jnp.where(it == k, weights[k][which], value)
        return value

    def near_product(leaf, j, where):
        i = leaf * near_count + j
        return dot3(near_h[i], near_l[i], win_h[where], win_l[where])

    def sub_copy(it, k, owner, target):
        return pltpu.make_async_remote_copy(
            src_ref=sub_all.at[it, owner],
            dst_ref=sub_all.at[it, owner],
            send_sem=sub_send.at[k],
            recv_sem=sub_recv.at[it, owner],
            device_id={"sub": target},
            device_id_type=MESH,
        )

    def iteration(it, carry):
        chain = c_chain(it)

        def own(leaf, carry):
            rows = pl.ds(leaf * leaf_rows, leaf_rows)
            residual[rows, :] = residual[rows, :] - (
                ridge_shift * update[leaf] + near_product(leaf, 0, REACH + leaf)
            )
            return carry

        for t in range(1, places):

            @pl.when(it > 0)
            def _():
                halo_start(it, t)
                chain.relay(t)

            begin, end = leaf_count * (t - 1) // (places - 1), leaf_count * t // (places - 1)
            if begin < end:
                lax.fori_loop(begin, end, own, 0)
        chain.finish()
        for b in range(n_clu):
            g_h[b], g_l[b] = split(coeffs[it, b])
        flat = (n_clu * rank, g_h.shape[2])
        sub_all[it, sub] = dot3(
            tt_h[...], tt_l[...], g_h[...].reshape(flat), g_l[...].reshape(flat)
        )
        for k in range(1, n_sub):
            sub_copy(it, k, sub, lax.rem(sub + k, n_sub)).start()
        far = None
        for j in range(ncc):
            at = jnp.clip(cluster_list[0, j] - sub * n_clu, 0, n_clu - 1)
            ah, al = split(cluster_coupling[0, j])
            term = dot3(ah, al, g_h[at], g_l[at])
            far = term if far is None else far + term
        c_far[...] = far

        def arrive(side):
            for piece in range(HALO_PIECES):
                halo_copy(it, side, piece).wait_recv()
            base = 0 if side == 0 else REACH + leaf_count

            @pl.when(it == 0)
            def _():
                for k in range(REACH):
                    win_h[base + k], win_l[base + k] = split(halo[it, side, k])

            @pl.when(it == 1)
            def _():
                w_copy(side).wait_recv()
                for k in range(REACH):
                    wb_h[side, k], wb_l[side, k] = split(w_beside[side, k])

            @pl.when(it >= 1)
            def _():
                past = it - 1
                down_copy(past, side).wait_recv()
                gain = pick_weight(past, 1)
                dh, dl = split(down_beside[past, side])
                for k in range(REACH):
                    far = dot3(wb_h[side, k], wb_l[side, k], dh, dl)
                    win_h[base + k], win_l[base + k] = split(halo[it, side, k] - gain * far)

        @pl.when(has_low)
        def _():
            arrive(0)

        @pl.when(has_high)
        def _():
            arrive(1)

        @pl.when(it == 0)
        def _():
            both_sides(lambda side: w_copy(side).start())

        def others(leaf, carry):
            rows = pl.ds(leaf * leaf_rows, leaf_rows)
            total = None
            for j in range(1, near_count):
                where = jnp.clip(near_index[leaf, j] - first_leaf + REACH, 0, win_h.shape[0] - 1)
                term = near_product(leaf, j, where)
                total = term if total is None else total + term
            residual[rows, :] = residual[rows, :] - total
            return carry

        lax.fori_loop(0, leaf_count, others, 0)

        keep, gain = pick_weight(it, 0), pick_weight(it, 1)

        def sent(side):
            for piece in range(HALO_PIECES):
                halo_copy(it, side, piece).wait_send()

        both_sides(sent)

        @pl.when(it >= 1)
        def _():
            both_sides(lambda side: down_copy(it - 1, side).wait_send())

        @pl.when(it == 1)
        def _():
            both_sides(lambda side: w_copy(side).wait_send())

        @pl.when(it + 1 < ITERS)
        def _():
            def advance(leaf, carry):
                rows = pl.ds(leaf * leaf_rows, leaf_rows)
                u = keep * update[leaf] + gain * residual[rows, :]
                pending[leaf] = u
                win_h[REACH + leaf], win_l[REACH + leaf] = split(u)
                return carry

            lax.fori_loop(0, leaf_count, advance, 0)
            halo_start(it + 1, 0)
            c_near[...] = own_coeffs()

        for k in range(1, n_sub):
            owner = lax.rem(sub + k, n_sub)
            sub_copy(it, k, owner, owner).wait_recv()
        for s in range(n_sub):
            s_h[s], s_l[s] = split(sub_all[it, s])
        top = None
        for j in range(nsc):
            at = subtree_list[0, j]
            ah, al = split(subtree_coupling[0, j])
            term = dot3(ah, al, s_h[at], s_l[at])
            top = term if top is None else top + term
        th, tl = split(top)
        ch, cl = split(cluster_transfer[0])
        down = c_far[...] + dot3(ch, cl, th, tl)
        down_h[...], down_l[...] = split(down)

        chain.drain()
        for k in range(1, n_sub):
            sub_copy(it, k, sub, lax.rem(sub + k, n_sub)).wait_send()

        def far_of(leaf):
            return dot3(w_h[leaf], w_l[leaf], down_h[...], down_l[...])

        @pl.when(it + 1 < ITERS)
        def _():
            gh, gl = split(gram[...])
            coeffs[it + 1, clu] = c_near[...] - gain * dot3(gh, gl, down_h[...], down_l[...])
            c_chain(it + 1).begin()
            down_own[it] = down
            both_sides(lambda side: down_copy(it, side).start())

            def finish(leaf, carry):
                rows = pl.ds(leaf * leaf_rows, leaf_rows)
                far = far_of(leaf)
                residual[rows, :] = residual[rows, :] - far
                u = pending[leaf] - gain * far
                update[leaf] = u
                solution[rows, :] = solution[rows, :] + u
                win_h[REACH + leaf], win_l[REACH + leaf] = split(u)
                return carry

            lax.fori_loop(0, leaf_count, finish, 0)

        @pl.when(it + 1 == ITERS)
        def _():
            def finish(leaf, carry):
                rows = pl.ds(leaf * leaf_rows, leaf_rows)
                residual[rows, :] = residual[rows, :] - far_of(leaf)
                return carry

            lax.fori_loop(0, leaf_count, finish, 0)

        return carry

    lax.fori_loop(0, ITERS, iteration, 0)


def body(
    right_side,
    near_blocks,
    near_index,
    bases,
    leaf_transfer,
    cluster_transfer,
    cluster_coupling,
    cluster_list,
    subtree_coupling,
    subtree_list,
):
    n_clu, n_sub = lax.axis_size("clu"), lax.axis_size("sub")
    leaf_count, leaf_rows, rank = bases.shape
    columns = right_side.shape[1]
    near_count = near_index.shape[1]
    blocks = leaf_count * near_count
    wide = leaf_count + 2 * REACH
    f32, bf16 = jnp.float32, jnp.bfloat16
    vmem = pl.BlockSpec(memory_space=pltpu.VMEM)
    smem = pl.BlockSpec(memory_space=pltpu.SMEM)
    hbm = pl.BlockSpec(memory_space=pl.ANY)
    dma = pltpu.SemaphoreType.DMA

    def run(*args):
        return kernel(n_clu, n_sub, *args)

    return pl.pallas_call(
        run,
        out_shape=(
            jax.ShapeDtypeStruct(right_side.shape, f32),
            jax.ShapeDtypeStruct(right_side.shape, f32),
        ),
        in_specs=[smem] * 3 + [vmem, hbm] + [vmem] * 5,
        out_specs=(vmem, vmem),
        scratch_shapes=[
            pltpu.VMEM((leaf_count, leaf_rows, columns), f32),
            pltpu.VMEM((ITERS, 2, REACH, leaf_rows, columns), f32),
            pltpu.VMEM((wide, leaf_rows, columns), bf16),
            pltpu.VMEM((wide, leaf_rows, columns), bf16),
            pltpu.VMEM((2, leaf_rows, leaf_rows), f32),
            pltpu.VMEM((blocks, leaf_rows, leaf_rows), bf16),
            pltpu.VMEM((blocks, leaf_rows, leaf_rows), bf16),
            pltpu.VMEM((leaf_count, leaf_rows, rank), bf16),
            pltpu.VMEM((leaf_count, leaf_rows, rank), bf16),
            pltpu.VMEM((leaf_count, rank, leaf_rows), bf16),
            pltpu.VMEM((leaf_count, rank, leaf_rows), bf16),
            pltpu.VMEM((n_clu, rank, rank), f32),
            pltpu.VMEM((rank, n_clu * rank), bf16),
            pltpu.VMEM((rank, n_clu * rank), bf16),
            pltpu.VMEM((ITERS, n_clu, rank, columns), f32),
            pltpu.VMEM((n_clu, rank, columns), bf16),
            pltpu.VMEM((n_clu, rank, columns), bf16),
            pltpu.VMEM((ITERS, n_sub, rank, columns), f32),
            pltpu.VMEM((n_sub, rank, columns), bf16),
            pltpu.VMEM((n_sub, rank, columns), bf16),
            pltpu.VMEM((rank, columns), f32),
            pltpu.VMEM((rank, columns), f32),
            pltpu.VMEM((rank, rank), f32),
            pltpu.VMEM((rank, columns), bf16),
            pltpu.VMEM((rank, columns), bf16),
            pltpu.VMEM((leaf_count, leaf_rows, columns), f32),
            pltpu.VMEM((leaf_count, leaf_rows, rank), f32),
            pltpu.VMEM((2, REACH, leaf_rows, rank), f32),
            pltpu.VMEM((2, REACH, leaf_rows, rank), bf16),
            pltpu.VMEM((2, REACH, leaf_rows, rank), bf16),
            pltpu.VMEM((ITERS - 1, rank, columns), f32),
            pltpu.VMEM((ITERS - 1, 2, rank, columns), f32),
            dma((2,)),
            dma((2, HALO_PIECES)),
            dma((ITERS, 2, HALO_PIECES)),
            dma((3, n_clu, PIECES)),
            dma((n_clu, PIECES)),
            dma((3, n_clu, PIECES)),
            dma((ITERS, n_clu, PIECES)),
            dma((n_sub,)),
            dma((ITERS, n_sub)),
            dma((2,)),
            dma((2,)),
            dma((2,)),
            dma((ITERS - 1, 2)),
        ],
        compiler_params=pltpu.CompilerParams(
            collective_id=0, has_side_effects=True, vmem_limit_bytes=63_000_000
        ),
    )(
        near_index,
        cluster_list,
        subtree_list,
        right_side,
        near_blocks,
        bases,
        leaf_transfer,
        cluster_transfer,
        cluster_coupling,
        subtree_coupling,
    )


def solution(mesh):
    placed = (
        P(("sub", "clu"), None),
        P(("sub", "clu"), None, None, None),
        P(("sub", "clu"), None),
        P(("sub", "clu"), None, None),
        P(("sub", "clu"), None, None),
        P(("sub", "clu"), None, None),
        P(("sub", "clu"), None, None, None),
        P(("sub", "clu"), None),
        P("sub", None, None, None),
        P("sub", None),
    )
    return jax.shard_map(
        body,
        mesh=mesh,
        in_specs=placed,
        out_specs=(P(("sub", "clu"), None), P(("sub", "clu"), None)),
        check_vma=False,
    )
```
